32 devices in a mesh: rep: 4 (over z), shard: 2 (over x), tp: 4 (over y, core).
Axes of the slice: x: 2, y: 2, z: 4, core: 2. Of those that a mesh axis runs over, the one named last changes fastest.
Arguments:
- inner_dense: float32 [4, 2, 768, 3072], P('rep', None, 'shard', 'tp'), may hold values from -6 to 6
- inner_emb: float32 [4, 8192, 768], P('rep', ('shard', 'tp')), may hold values from -6 to 6
- outer_dense: float32 [2, 2, 384, 3072], P(None, 'shard', ('rep', 'tp')), may hold values from -6 to 6
- moment_dense: float32 [2, 2, 384, 3072], P(None, 'shard', ('rep', 'tp')), may hold values from -3 to 3
- outer_emb: float32 [2, 4, 16, 64, 768], P('shard', None, ('rep', 'tp')), may hold values from -6 to 6
- moment_emb: float32 [2, 4, 16, 64, 768], P('shard', None, ('rep', 'tp')), may hold values from -3 to 3
- basis: float32 [64, 768], replicated, may hold values from -0.1875 to 0.1875
Outputs:
- new_outer_dense: float32 [2, 2, 384, 3072], P(None, 'shard', ('rep', 'tp'))
- new_moment_dense: float32 [2, 2, 384, 3072], P(None, 'shard', ('rep', 'tp'))
- new_outer_emb: float32 [2, 4, 16, 64, 768], P('shard', None, ('rep', 'tp'))
- new_moment_emb: float32 [2, 4, 16, 64, 768], P('shard', None, ('rep', 'tp'))
- train_dense: float32 [2, 768, 3072], P(None, 'shard', 'tp')
- train_emb: float32 [8192, 768], P(('shard', 'tp'))
The draws below stay inside these ranges and needn't reach their ends.
All inputs are finite; a program needn't handle non-finite values.
Results may differ from the reference program's by a relative error of at most 0.00007.
Values sent between devices are 32-bit elements; how exact they have to be, the bound alone decides.
No kernel may reach another device: no remote copies, remote signals or barrier semaphores. Data moves between devices by JAX's collectives and lax.ppermute only.
A program may use at most 64 MiB of HBM per device.

```python
import jax
import jax.numpy as jnp
from jax import lax

D = 768
FF = 3072
RANK = 64
EMB_SHARD = 4096
VOCAB = 8192
N_REP = 4
N_SHARD = 2
N_TP = 4


def block_levels(stream_key, shape, pieces, least, top_value):
    def one(dim, blocks):
        draws = jax.random.uniform(jax.random.fold_in(jax.random.fold_in(stream_key, 6), dim), (blocks,), jnp.float32, least / len(pieces), top_value / len(pieces))
        return jnp.repeat(jnp.exp(draws), shape[dim] // blocks).reshape((-1,) + (1,) * (len(shape) - dim - 1))

    level = one(*pieces[0])
    for cut in pieces[1:]:
        level = level * one(*cut)
    return level


def noise(rng, extent, scale, bound, cuts=(), dtype=jnp.bfloat16):
    entries = jax.random.normal(rng, extent, jnp.float32) * scale
    if len(cuts) > 0:
        entries = block_levels(rng, extent, cuts, -0.22, 0.18) * entries
    return jnp.clip(entries, min=-bound, max=bound).astype(dtype)


def setup_inputs(seed: int = 0) -> dict:
    streams_of = jax.random.split(jax.random.key(seed), 8)
    inner_dense = noise(streams_of[0], (N_REP, 2, D, FF), 1.0, 6.0, ((0, 4), (2, 2), (3, 4)), jnp.float32)
    inner_emb = noise(streams_of[1], (N_REP, VOCAB, D), 1.0, 6.0, ((0, 4), (1, 8)), jnp.float32)
    outer_dense = noise(streams_of[2], (2, N_SHARD, D // N_SHARD, FF), 1.0, 6.0, ((1, 2), (2, 16)), jnp.float32)
    moment_dense = noise(streams_of[3], (2, N_SHARD, D // N_SHARD, FF), 0.5, 3.0, ((1, 2), (2, 16)), jnp.float32)
    outer_emb = noise(streams_of[4], (N_SHARD, N_TP, N_REP * N_TP, EMB_SHARD // (N_REP * N_TP * N_TP), D), 1.0, 6.0, ((0, 2), (2, 16)), jnp.float32)
    moment_emb = noise(streams_of[5], (N_SHARD, N_TP, N_REP * N_TP, EMB_SHARD // (N_REP * N_TP * N_TP), D), 0.5, 3.0, ((0, 2), (2, 16)), jnp.float32)
    basis = noise(streams_of[6], (RANK, D), (16 * RANK) ** -0.5, 0.1875, (), jnp.float32)
    return dict(inner_dense=inner_dense, inner_emb=inner_emb, outer_dense=outer_dense, moment_dense=moment_dense, outer_emb=outer_emb, moment_emb=moment_emb, basis=basis)


momentum = 0.9
outer_rate = 0.7


def reference(inner_dense, inner_emb, outer_dense, moment_dense, outer_emb, moment_emb, basis):
    groups = inner_dense.shape[0]
    dense_flat = outer_dense.reshape(2, D, FF)
    dense_moment = moment_dense.reshape(2, D, FF)
    grad_dense = dense_flat - jnp.sum(inner_dense, axis=0) / groups
    emb_flat = outer_emb.reshape(VOCAB, D)
    emb_moment = moment_emb.reshape(VOCAB, D)
    emb_diff = emb_flat - jnp.sum(inner_emb, axis=0) / groups
    factors = jnp.dot(emb_diff, basis.T, precision=lax.Precision.HIGHEST, preferred_element_type=jnp.float32)
    grad_emb = jnp.dot(factors, basis, precision=lax.Precision.HIGHEST, preferred_element_type=jnp.float32)
    moment_new = momentum * dense_moment + grad_dense
    dense_new = dense_flat - outer_rate * (grad_dense + momentum * moment_new)
    emb_moment_new = momentum * emb_moment + grad_emb
    emb_new = emb_flat - outer_rate * (grad_emb + momentum * emb_moment_new)
    return (dense_new.reshape(outer_dense.shape), moment_new.reshape(outer_dense.shape),
            emb_new.reshape(outer_emb.shape), emb_moment_new.reshape(outer_emb.shape),
            dense_new, emb_new)
```

```python
import jax
import jax.numpy as jnp
from jax import lax
from jax.sharding import PartitionSpec as P

momentum = 0.9
outer_rate = 0.7
grad_weight = outer_rate * (1.0 + momentum)
moment_weight = outer_rate * momentum * momentum


def dot(a, b):
    return jnp.dot(a, b, precision=lax.Precision.HIGHEST, preferred_element_type=jnp.float32)


def pack(f, pieces):
    half = f.shape[0] // pieces // 2
    f = f.reshape(pieces, 2, half, f.shape[1])
    return jnp.concatenate([f[:, 0], f[:, 1]], axis=-1)


def unpack(f):
    k = f.shape[-1] // 2
    return jnp.concatenate([f[..., :k], f[..., k:]], axis=1)


def swap_tp(pieces):
    count = lax.axis_size("tp")
    me = lax.axis_index("tp")
    got = []
    for d in range(count):
        piece = lax.dynamic_index_in_dim(pieces, me ^ d, 0, keepdims=False)
        if d:
            piece = lax.ppermute(piece, "tp", [(i, i ^ d) for i in range(count)])
        got.append(piece)
    ordered = []
    for j in range(count):
        out = got[j]
        for i in range(1, count):
            out = jnp.where(me == i, got[j ^ i], out)
        ordered.append(out)
    return jnp.stack(ordered)


def per_device(inner_dense, inner_emb, outer_dense, moment_dense, outer_emb, moment_emb, basis):
    groups = lax.axis_size("rep")
    tp_count = lax.axis_size("tp")
    me = lax.axis_index("rep")
    up = [(i, (i + 1) % groups) for i in range(groups)]
    down = [((i + 1) % groups, i) for i in range(groups)]
    two = [(i, (i + 2) % groups) for i in range(groups)]

    def after(i):
        return lax.rem(me + groups + i, groups)

    def send(x, pairs):
        return lax.ppermute(x, "rep", pairs)

    width = basis.shape[1]
    dense = inner_dense[0]
    cols = dense.shape[2]
    block_rows = dense.shape[1] // groups
    flat_rows = outer_dense.shape[2]
    piece_rows = outer_emb.shape[3]
    emb_rows = tp_count * piece_rows

    def block(i, h):
        return lax.dynamic_slice(dense, (h, after(i) * block_rows, 0), (1, block_rows, cols))[0]

    far_up = send(block(2, 0), up)
    far_down = send(block(2, 1), down)
    near_up = send(block(1, 1), up)
    near_down = send(block(-1, 0), down)

    projected = pack(dot(inner_emb[0], basis.T), groups * tp_count)
    projected = projected.reshape((groups, tp_count) + projected.shape[1:])

    def part(i):
        return lax.dynamic_index_in_dim(projected, after(i), 0, keepdims=False)

    proj_sum = part(0) + send(part(1), up) + send(part(-1), down) + send(part(2), two)

    emb_outer = outer_emb[0, :, 0]
    emb_moment = moment_emb[0, :, 0]
    outer_proj = dot(emb_outer.reshape(-1, width), basis.T)
    outer_grad = dot(outer_proj, basis).reshape(emb_outer.shape)
    emb_base = swap_tp(emb_outer - moment_weight * emb_moment - grad_weight * outer_grad)
    dense_outer = outer_dense[:, 0]
    dense_moment = moment_dense[:, 0]
    dense_base = (1.0 - grad_weight) * dense_outer - moment_weight * dense_moment
    dense_base = swap_tp(
        dense_base.reshape(2, flat_rows, tp_count, cols).transpose(2, 0, 1, 3)
    ).transpose(1, 0, 2, 3).reshape(2, block_rows, cols)

    sum_up = send(block(1, 0) + far_up, up)
    sum_down = send(block(-1, 1) + far_down, down)
    dense_sum = (block(0, 0) + near_down + sum_up, block(0, 1) + near_up + sum_down)

    emb_block = emb_base.reshape(emb_rows, width) + (grad_weight / groups) * dot(
        unpack(proj_sum).reshape(emb_rows, -1), basis
    )
    emb_half = emb_rows // 2
    emb_parts = (emb_block[:emb_half], emb_block[emb_half:])
    dense_parts = tuple(dense_base[h] + (grad_weight / groups) * dense_sum[h] for h in (0, 1))

    def gather(parts):
        left0 = send(parts[0], up)
        right1 = send(parts[1], down)
        left1 = send(parts[1], up)
        right0 = send(parts[0], down)
        far0 = send(left0, up)
        far1 = send(right1, down)
        return {0: parts, -1: (left0, left1), 1: (right0, right1), 2: (far0, far1)}

    emb_all = gather(emb_parts)
    dense_all = gather(dense_parts)
    embed_train = jnp.zeros((groups * emb_rows, width), jnp.float32)
    for i, halves in emb_all.items():
        for h, value in enumerate(halves):
            embed_train = lax.dynamic_update_slice(
                embed_train, value, (after(i) * emb_rows + h * emb_half, 0)
            )
    dense_train = jnp.zeros(dense.shape, jnp.float32)
    for i, halves in dense_all.items():
        for h, value in enumerate(halves):
            dense_train = lax.dynamic_update_slice(
                dense_train, value[None], (h, after(i) * block_rows, 0)
            )

    dense_back = swap_tp(
        jnp.stack(dense_sum).reshape(2, tp_count, flat_rows, cols).transpose(1, 0, 2, 3)
    ).transpose(1, 2, 0, 3).reshape(2, flat_rows, tp_count * cols)
    grad_dense = dense_outer - dense_back / groups
    moment_new = momentum * dense_moment + grad_dense
    dense_new = dense_outer - outer_rate * (grad_dense + momentum * moment_new)
    proj_back = unpack(swap_tp(proj_sum)).reshape(tp_count * piece_rows, -1)
    factors = outer_proj - proj_back / groups
    grad_emb = dot(factors, basis).reshape(emb_outer.shape)
    emb_moment_new = momentum * emb_moment + grad_emb
    emb_new = emb_outer - outer_rate * (grad_emb + momentum * emb_moment_new)
    return (
        dense_new[:, None],
        moment_new[:, None],
        emb_new[None, :, None],
        emb_moment_new[None, :, None],
        dense_train,
        embed_train,
    )


def solution(mesh):
    in_specs = (
        P("rep", None, "shard", "tp"),
        P("rep", ("shard", "tp"), None),
        P(None, "shard", ("rep", "tp"), None),
        P(None, "shard", ("rep", "tp"), None),
        P("shard", None, ("rep", "tp"), None, None),
        P("shard", None, ("rep", "tp"), None, None),
        P(),
    )
    out_specs = (
        P(None, "shard", ("rep", "tp"), None),
        P(None, "shard", ("rep", "tp"), None),
        P("shard", None, ("rep", "tp"), None, None),
        P("shard", None, ("rep", "tp"), None, None),
        P(None, "shard", "tp"),
        P(("shard", "tp"), None),
    )
    return jax.shard_map(
        per_device, mesh=mesh, in_specs=in_specs, out_specs=out_specs, check_vma=False
    )
```

```python
import functools

import jax
import jax.numpy as jnp
from jax import lax
from jax.experimental import pallas as pl
from jax.experimental.pallas import tpu as pltpu
from jax.sharding import PartitionSpec as P

momentum = 0.9
outer_rate = 0.7
grad_weight = outer_rate * (1.0 + momentum)
moment_weight = outer_rate * momentum * momentum
vmem_limit = 48 * 1024 * 1024
f32 = jnp.float32
any_spec = pl.BlockSpec(memory_space=pl.ANY)
vmem_spec = pl.BlockSpec(memory_space=pltpu.VMEM)


def mul_t(a, b):
    return lax.dot_general(
        a, b, (((1,), (1,)), ((), ())), precision=lax.Precision.HIGHEST, preferred_element_type=f32
    )


def mul(a, b):
    return jnp.dot(a, b, precision=lax.Precision.HIGHEST, preferred_element_type=f32)


def shaped(*shape):
    return jax.ShapeDtypeStruct(shape, f32)


def call(body, outs, n_in, scratch=(), flops=0, size=0):
    return pl.pallas_call(
        body,
        out_shape=outs,
        in_specs=[vmem_spec] * n_in,
        out_specs=jax.tree.map(lambda _: vmem_spec, outs),
        scratch_shapes=scratch,
        compiler_params=pltpu.CompilerParams(vmem_limit_bytes=vmem_limit),
        cost_estimate=pl.CostEstimate(flops=flops, bytes_accessed=size, transcendentals=0),
    )


def wide_basis(basis):
    zero = jnp.zeros_like(basis)
    return jnp.concatenate([basis, zero]), jnp.concatenate([zero, basis])


def project_body(count, groups, pieces, me_ref, x_ref, basis_ref, *out_refs):
    step = pl.program_id(0)
    first, second = wide_basis(basis_ref[...])
    rows, width = x_ref.shape[1:]
    x = x_ref[0].reshape(pieces, 2, rows // pieces // 2, width)
    y = mul_t(x[:, 0].reshape(-1, width), first) + mul_t(x[:, 1].reshape(-1, width), second)
    y = y.reshape(pieces, rows // pieces // 2, -1)
    for i in range(count):

        @pl.when(step == i)
        def _(i=i):
            out_refs[i][...] = y


def project(inner_emb, basis, me, groups, pieces):
    rows, width = inner_emb.shape[1] // groups, inner_emb.shape[2]
    rank = basis.shape[0]
    shape = (pieces, rows // pieces // 2, 2 * rank)

    def source(i, me):
        return 0, me[0] ^ (groups - 1 - i), 0

    return pl.pallas_call(
        functools.partial(project_body, 4, groups, pieces),
        out_shape=[shaped(*shape)] * 4,
        grid_spec=pltpu.PrefetchScalarGridSpec(
            num_scalar_prefetch=1,
            grid=(4,),
            in_specs=[
                pl.BlockSpec((1, rows, width), source),
                pl.BlockSpec((rank, width), lambda i, me: (0, 0)),
            ],
            out_specs=[pl.BlockSpec(shape, lambda i, me: (0, 0, 0))] * 4,
        ),
        compiler_params=pltpu.CompilerParams(vmem_limit_bytes=vmem_limit),
        cost_estimate=pl.CostEstimate(
            flops=12 * groups * rows * width * rank,
            bytes_accessed=4 * groups * rows * (width + rank),
            transcendentals=0,
        ),
    )(me, inner_emb, basis)


def emb_base_body(outer_ref, moment_ref, basis_ref, base_ref, proj_ref):
    shape = base_ref.shape
    outer = outer_ref[0, :, 0].reshape(-1, shape[-1])
    moment = moment_ref[0, :, 0].reshape(-1, shape[-1])
    basis = basis_ref[...]
    proj = mul_t(outer, basis)
    proj_ref[...] = proj
    base = outer - moment_weight * moment - grad_weight * mul(proj, basis)
    base_ref[...] = base.reshape(shape)


def emb_block_body(scale, base_ref, p0, p1, p2, p3, basis_ref, block_ref, sum_ref):
    total = p0[...] + p1[...] + p2[...] + p3[...]
    sum_ref[...] = total
    pieces, half, wide = total.shape
    flat = total.reshape(pieces * half, wide)
    first, second = wide_basis(basis_ref[...])
    base = base_ref[...]
    block_ref[:, 0] = base[:, 0] + scale * mul(flat, first).reshape(pieces, half, -1)
    block_ref[:, 1] = base[:, 1] + scale * mul(flat, second).reshape(pieces, half, -1)


def emb_state_body(scale, outer_ref, moment_ref, proj_ref, back_ref, basis_ref, new_ref, moment_new_ref):
    pieces, half, wide = back_ref.shape
    basis = basis_ref[...]
    first, second = wide_basis(basis)
    flat = back_ref[...].reshape(pieces * half, wide)
    outer = outer_ref[0, :, 0]
    width = outer.shape[-1]
    own = mul(proj_ref[...], basis).reshape(pieces, 2, half, width)
    grad = jnp.concatenate(
        [
            own[:, i : i + 1] - scale * mul(flat, part).reshape(pieces, 1, half, width)
            for i, part in ((0, first), (1, second))
        ],
        axis=1,
    ).reshape(outer.shape)
    moment_new = momentum * moment_ref[0, :, 0] + grad
    moment_new_ref[0, :, 0] = moment_new
    new_ref[0, :, 0] = outer - outer_rate * (grad + momentum * moment_new)


def per_device(inner_dense, inner_emb, outer_dense, moment_dense, outer_emb, moment_emb, basis):
    groups = lax.axis_size("rep")
    tp_count = lax.axis_size("tp")
    me = lax.axis_index("rep")

    def send(x, d):
        return lax.ppermute(x, "rep", [(i, i ^ d) for i in range(groups)])

    def meet(*xs):
        return lax.optimization_barrier(xs)

    def swap(x):
        return lax.all_to_all(x, "tp", split_axis=0, concat_axis=0, tiled=True)

    rank, width = basis.shape
    dense = inner_dense[0]
    cols = dense.shape[2]
    block_rows = dense.shape[1] // groups
    flat_rows = outer_dense.shape[2]
    piece_rows = outer_emb.shape[3]
    half_rows = piece_rows // 2
    emb_rows = tp_count * piece_rows
    weight = grad_weight / groups

    def block(d):
        return lax.dynamic_slice(dense, (0, (me ^ d) * block_rows, 0), (2, block_rows, cols))

    far, inner_emb, outer_emb, outer_dense = meet(block(3), inner_emb, outer_emb, outer_dense)
    far = send(far, 1)

    p3, p2, p1, p0 = project(inner_emb, basis, me.reshape(1).astype(jnp.int32), groups, tp_count)
    emb_base, outer_proj = call(
        emb_base_body,
        [shaped(tp_count, piece_rows, width), shaped(emb_rows, rank)],
        3,
        flops=24 * emb_rows * width * rank,
        size=12 * emb_rows * width,
    )(outer_emb, moment_emb, basis)
    far, p3, p2, p1, emb_base = meet(far, p3, p2, p1, emb_base)
    p3, p2, p1 = send(p3, 3), send(p2, 2), send(p1, 1)
    emb_base = swap(emb_base)
    across = send(block(2) + far, 2)
    near = send(block(1), 1)
    dense_outer = outer_dense[:, 0]
    dense_moment = moment_dense[:, 0]
    dense_base = (1.0 - grad_weight) * dense_outer - moment_weight * dense_moment
    dense_base = jnp.stack([dense_base[:, :, j * cols : (j + 1) * cols] for j in range(tp_count)])

    emb_block, proj_sum = call(
        functools.partial(emb_block_body, weight),
        [shaped(tp_count, 2, half_rows, width), shaped(tp_count, half_rows, 2 * rank)],
        6,
        flops=24 * emb_rows * width * rank,
        size=8 * emb_rows * width,
    )(emb_base.reshape(tp_count, 2, half_rows, width), p0, p1, p2, p3, basis)
    emb_block, proj_sum, dense_base = meet(emb_block, proj_sum, dense_base)
    dense_base = swap(dense_base)
    across, near, emb_block = meet(across, near, emb_block)
    dense_sum = block(0) + near + across
    emb_block = emb_block.reshape(emb_rows, width)
    dense_block = (
        dense_base.transpose(1, 0, 2, 3).reshape(2, block_rows, cols) + weight * dense_sum
    )

    def gather(x):
        second = send(x, 2)
        first = send(x, 1)
        return x, first, second, send(second, 1)

    emb_all = gather(emb_block)
    dense_all = gather(dense_block)
    embed_train = jnp.zeros((groups * emb_rows, width), f32)
    for d, value in enumerate(emb_all):
        embed_train = lax.dynamic_update_slice(embed_train, value, ((me ^ d) * emb_rows, 0))
    dense_train = jnp.zeros(dense.shape, f32)
    for d, value in enumerate(dense_all):
        dense_train = lax.dynamic_update_slice(dense_train, value, (0, (me ^ d) * block_rows, 0))

    dense_back = swap(dense_sum.reshape(2, tp_count, flat_rows, cols).transpose(1, 0, 2, 3))
    dense_back = jnp.concatenate([dense_back[j] for j in range(tp_count)], axis=-1)
    grad_dense = dense_outer - dense_back / groups
    moment_new = momentum * dense_moment + grad_dense
    dense_new = dense_outer - outer_rate * (grad_dense + momentum * moment_new)
    emb_new, emb_moment_new = call(
        functools.partial(emb_state_body, 1.0 / groups),
        [shaped(*outer_emb.shape)] * 2,
        5,
        flops=36 * emb_rows * width * rank,
        size=16 * emb_rows * width,
    )(outer_emb, moment_emb, outer_proj, swap(proj_sum), basis)
    return (
        dense_new[:, None],
        moment_new[:, None],
        emb_new,
        emb_moment_new,
        dense_train,
        embed_train,
    )


def solution(mesh):
    in_specs = (
        P("rep", None, "shard", "tp"),
        P("rep", ("shard", "tp"), None),
        P(None, "shard", ("rep", "tp"), None),
        P(None, "shard", ("rep", "tp"), None),
        P("shard", None, ("rep", "tp"), None, None),
        P("shard", None, ("rep", "tp"), None, None),
        P(),
    )
    out_specs = (
        P(None, "shard", ("rep", "tp"), None),
        P(None, "shard", ("rep", "tp"), None),
        P("shard", None, ("rep", "tp"), None, None),
        P("shard", None, ("rep", "tp"), None, None),
        P(None, "shard", "tp"),
        P(("shard", "tp"), None),
    )
    return jax.shard_map(
        per_device, mesh=mesh, in_specs=in_specs, out_specs=out_specs, check_vma=False
    )
```

```python
import functools

import jax
import jax.numpy as jnp
from jax import lax
from jax.experimental import pallas as pl
from jax.experimental.pallas import tpu as pltpu
from jax.sharding import PartitionSpec as P

momentum = 0.9
outer_rate = 0.7
grad_weight = outer_rate * (1.0 + momentum)
moment_weight = outer_rate * momentum * momentum
vmem_limit = 48 * 1024 * 1024
f32 = jnp.float32
any_spec = pl.BlockSpec(memory_space=pl.ANY)
vmem_spec = pl.BlockSpec(memory_space=pltpu.VMEM)


def mul_t(a, b):
    return lax.dot_general(
        a, b, (((1,), (1,)), ((), ())), precision=lax.Precision.HIGHEST, preferred_element_type=f32
    )


def mul(a, b):
    return jnp.dot(a, b, precision=lax.Precision.HIGHEST, preferred_element_type=f32)


def shaped(*shape):
    return jax.ShapeDtypeStruct(shape, f32)


def call(body, outs, n_in, scratch=(), flops=0, size=0):
    return pl.pallas_call(
        body,
        out_shape=outs,
        in_specs=[vmem_spec] * n_in,
        out_specs=jax.tree.map(lambda _: vmem_spec, outs),
        scratch_shapes=scratch,
        compiler_params=pltpu.CompilerParams(vmem_limit_bytes=vmem_limit),
        cost_estimate=pl.CostEstimate(flops=0, bytes_accessed=0, transcendentals=0),
    )


def wide_basis(basis):
    zero = jnp.zeros_like(basis)
    return jnp.concatenate([basis, zero]), jnp.concatenate([zero, basis])


def project_body(count, groups, pieces, me_ref, x_ref, basis_ref, *out_refs):
    step = pl.program_id(0)
    first, second = wide_basis(basis_ref[...])
    rows, width = x_ref.shape[1:]
    x = x_ref[0].reshape(pieces, 2, rows // pieces // 2, width)
    y = mul_t(x[:, 0].reshape(-1, width), first) + mul_t(x[:, 1].reshape(-1, width), second)
    y = y.reshape(pieces, rows // pieces // 2, -1)
    for i in range(count):

        @pl.when(step == i)
        def _(i=i):
            out_refs[i][...] = y


def project(inner_emb, basis, me, groups, pieces):
    rows, width = inner_emb.shape[1] // groups, inner_emb.shape[2]
    rank = basis.shape[0]
    shape = (pieces, rows // pieces // 2, 2 * rank)

    def source(i, me):
        return 0, me[0] ^ (groups - 1 - i), 0

    return pl.pallas_call(
        functools.partial(project_body, 4, groups, pieces),
        out_shape=[shaped(*shape)] * 4,
        grid_spec=pltpu.PrefetchScalarGridSpec(
            num_scalar_prefetch=1,
            grid=(4,),
            in_specs=[
                pl.BlockSpec((1, rows, width), source),
                pl.BlockSpec((rank, width), lambda i, me: (0, 0)),
            ],
            out_specs=[pl.BlockSpec(shape, lambda i, me: (0, 0, 0))] * 4,
        ),
        compiler_params=pltpu.CompilerParams(vmem_limit_bytes=vmem_limit),
        cost_estimate=pl.CostEstimate(
            flops=0,
            bytes_accessed=0,
            transcendentals=0,
        ),
    )(me, inner_emb, basis)


def emb_base_body(outer_ref, moment_ref, basis_ref, base_ref, proj_ref):
    shape = base_ref.shape
    outer = outer_ref[0, :, 0].reshape(-1, shape[-1])
    moment = moment_ref[0, :, 0].reshape(-1, shape[-1])
    basis = basis_ref[...]
    proj = mul_t(outer, basis)
    proj_ref[...] = proj
    base = outer - moment_weight * moment - grad_weight * mul(proj, basis)
    base_ref[...] = base.reshape(shape)


def emb_block_body(scale, base_ref, p0, p1, p2, p3, basis_ref, block_ref, sum_ref):
    total = p0[...] + p1[...] + p2[...] + p3[...]
    sum_ref[...] = total
    pieces, half, wide = total.shape
    flat = total.reshape(pieces * half, wide)
    first, second = wide_basis(basis_ref[...])
    base = base_ref[...]
    block_ref[:, 0] = base[:, 0] + scale * mul(flat, first).reshape(pieces, half, -1)
    block_ref[:, 1] = base[:, 1] + scale * mul(flat, second).reshape(pieces, half, -1)


def emb_state_body(scale, outer_ref, moment_ref, proj_ref, back_ref, basis_ref, new_ref, moment_new_ref):
    pieces, half, wide = back_ref.shape
    basis = basis_ref[...]
    first, second = wide_basis(basis)
    flat = back_ref[...].reshape(pieces * half, wide)
    outer = outer_ref[0, :, 0]
    width = outer.shape[-1]
    own = mul(proj_ref[...], basis).reshape(pieces, 2, half, width)
    grad = jnp.concatenate(
        [
            own[:, i : i + 1] - scale * mul(flat, part).reshape(pieces, 1, half, width)
            for i, part in ((0, first), (1, second))
        ],
        axis=1,
    ).reshape(outer.shape)
    moment_new = momentum * moment_ref[0, :, 0] + grad
    moment_new_ref[0, :, 0] = moment_new
    new_ref[0, :, 0] = outer - outer_rate * (grad + momentum * moment_new)


def per_device(inner_dense, inner_emb, outer_dense, moment_dense, outer_emb, moment_emb, basis):
    groups = lax.axis_size("rep")
    tp_count = lax.axis_size("tp")
    me = lax.axis_index("rep")

    def send(x, d):
        return lax.ppermute(x, "rep", [(i, i ^ d) for i in range(groups)])

    def meet(*xs):
        return lax.optimization_barrier(xs)

    def swap(x):
        return lax.all_to_all(x, "tp", split_axis=0, concat_axis=0, tiled=True)

    rank, width = basis.shape
    dense = inner_dense[0]
    cols = dense.shape[2]
    block_rows = dense.shape[1] // groups
    flat_rows = outer_dense.shape[2]
    piece_rows = outer_emb.shape[3]
    half_rows = piece_rows // 2
    emb_rows = tp_count * piece_rows
    weight = grad_weight / groups

    def block(d):
        return lax.dynamic_slice(dense, (0, (me ^ d) * block_rows, 0), (2, block_rows, cols))

    far, inner_emb, outer_emb, outer_dense, dense = meet(
        block(3), inner_emb, outer_emb, outer_dense, dense
    )
    far = send(far, 1)

    p3, p2, p1, p0 = project(inner_emb, basis, me.reshape(1).astype(jnp.int32), groups, tp_count)
    p3, p2, p1, p0, outer_emb = meet(p3, p2, p1, p0, outer_emb)
    p3, p2, p1 = send(p3, 3), send(p2, 2), send(p1, 1)
    emb_base, outer_proj = call(
        emb_base_body,
        [shaped(tp_count, piece_rows, width), shaped(emb_rows, rank)],
        3,
        flops=24 * emb_rows * width * rank,
        size=12 * emb_rows * width,
    )(outer_emb, moment_emb, basis)
    own, near, second = block(0), block(1), block(2)
    far, p3, p2, p1, emb_base, near = meet(far, p3, p2, p1, emb_base, near)
    emb_base = swap(emb_base)
    across = send(second + far, 2)
    near = send(near, 1)
    dense_outer = outer_dense[:, 0]
    dense_moment = moment_dense[:, 0]
    dense_base = (1.0 - grad_weight) * dense_outer - moment_weight * dense_moment
    dense_base = jnp.stack([dense_base[:, :, j * cols : (j + 1) * cols] for j in range(tp_count)])

    emb_block, proj_sum = call(
        functools.partial(emb_block_body, weight),
        [shaped(tp_count, 2, half_rows, width), shaped(tp_count, half_rows, 2 * rank)],
        6,
        flops=24 * emb_rows * width * rank,
        size=8 * emb_rows * width,
    )(emb_base.reshape(tp_count, 2, half_rows, width), p0, p1, p2, p3, basis)
    emb_block, proj_sum, dense_base = meet(emb_block, proj_sum, dense_base)
    dense_base = swap(dense_base)
    across, near, emb_block = meet(across, near, emb_block)
    dense_sum = own + near + across
    emb_block = emb_block.reshape(emb_rows, width)
    dense_block = (
        dense_base.transpose(1, 0, 2, 3).reshape(2, block_rows, cols) + weight * dense_sum
    )

    def gather(x):
        second = send(x, 2)
        first = send(x, 1)
        return x, first, second, send(second, 1)

    emb_all = gather(emb_block)
    dense_all = gather(dense_block)
    embed_train = jnp.zeros((groups * emb_rows, width), f32)
    for d, value in enumerate(emb_all):
        embed_train = lax.dynamic_update_slice(embed_train, value, ((me ^ d) * emb_rows, 0))
    dense_train = jnp.zeros(dense.shape, f32)
    for d, value in enumerate(dense_all):
        dense_train = lax.dynamic_update_slice(dense_train, value, (0, (me ^ d) * block_rows, 0))

    dense_back = swap(dense_sum.reshape(2, tp_count, flat_rows, cols).transpose(1, 0, 2, 3))
    dense_back = jnp.concatenate([dense_back[j] for j in range(tp_count)], axis=-1)
    grad_dense = dense_outer - dense_back / groups
    moment_new = momentum * dense_moment + grad_dense
    dense_new = dense_outer - outer_rate * (grad_dense + momentum * moment_new)
    emb_new, emb_moment_new = call(
        functools.partial(emb_state_body, 1.0 / groups),
        [shaped(*outer_emb.shape)] * 2,
        5,
        flops=36 * emb_rows * width * rank,
        size=16 * emb_rows * width,
    )(outer_emb, moment_emb, outer_proj, swap(proj_sum), basis)
    return (
        dense_new[:, None],
        moment_new[:, None],
        emb_new,
        emb_moment_new,
        dense_train,
        embed_train,
    )


def solution(mesh):
    in_specs = (
        P("rep", None, "shard", "tp"),
        P("rep", ("shard", "tp"), None),
        P(None, "shard", ("rep", "tp"), None),
        P(None, "shard", ("rep", "tp"), None),
        P("shard", None, ("rep", "tp"), None, None),
        P("shard", None, ("rep", "tp"), None, None),
        P(),
    )
    out_specs = (
        P(None, "shard", ("rep", "tp"), None),
        P(None, "shard", ("rep", "tp"), None),
        P("shard", None, ("rep", "tp"), None, None),
        P("shard", None, ("rep", "tp"), None, None),
        P(None, "shard", "tp"),
        P(("shard", "tp"), None),
    )
    return jax.shard_map(
        per_device, mesh=mesh, in_specs=in_specs, out_specs=out_specs, check_vma=False
    )
```

```python
import functools

import jax
import jax.numpy as jnp
from jax import lax
from jax.experimental import pallas as pl
from jax.experimental.pallas import tpu as pltpu
from jax.sharding import PartitionSpec as P

momentum = 0.9
outer_rate = 0.7
grad_weight = outer_rate * (1.0 + momentum)
moment_weight = outer_rate * momentum * momentum
vmem_limit = 48 * 1024 * 1024
f32 = jnp.float32
any_spec = pl.BlockSpec(memory_space=pl.ANY)
vmem_spec = pl.BlockSpec(memory_space=pltpu.VMEM)


def mul_t(a, b):
    return lax.dot_general(
        a, b, (((1,), (1,)), ((), ())), precision=lax.Precision.HIGHEST, preferred_element_type=f32
    )


def mul(a, b):
    return jnp.dot(a, b, precision=lax.Precision.HIGHEST, preferred_element_type=f32)


def shaped(*shape):
    return jax.ShapeDtypeStruct(shape, f32)


def call(body, outs, n_in, scratch=(), flops=0, size=0):
    return pl.pallas_call(
        body,
        out_shape=outs,
        in_specs=[vmem_spec] * n_in,
        out_specs=jax.tree.map(lambda _: vmem_spec, outs),
        scratch_shapes=scratch,
        compiler_params=pltpu.CompilerParams(vmem_limit_bytes=vmem_limit),
        cost_estimate=pl.CostEstimate(flops=0, bytes_accessed=0, transcendentals=0),
    )


def wide_basis(basis):
    zero = jnp.zeros_like(basis)
    return jnp.concatenate([basis, zero]), jnp.concatenate([zero, basis])


def project_body(count, groups, pieces, me_ref, x_ref, basis_ref, *out_refs):
    step = pl.program_id(0)
    first, second = wide_basis(basis_ref[...])
    rows, width = x_ref.shape[1:]
    x = x_ref[0].reshape(pieces, 2, rows // pieces // 2, width)
    y = mul_t(x[:, 0].reshape(-1, width), first) + mul_t(x[:, 1].reshape(-1, width), second)
    y = y.reshape(pieces, rows // pieces // 2, -1)
    for i in range(count):

        @pl.when(step == i)
        def _(i=i):
            out_refs[i][...] = y


def project(inner_emb, basis, me, groups, pieces):
    rows, width = inner_emb.shape[1] // groups, inner_emb.shape[2]
    rank = basis.shape[0]
    shape = (pieces, rows // pieces // 2, 2 * rank)

    def source(i, me):
        return 0, me[0] ^ (groups - 1 - i), 0

    return pl.pallas_call(
        functools.partial(project_body, 4, groups, pieces),
        out_shape=[shaped(*shape)] * 4,
        grid_spec=pltpu.PrefetchScalarGridSpec(
            num_scalar_prefetch=1,
            grid=(4,),
            in_specs=[
                pl.BlockSpec((1, rows, width), source),
                pl.BlockSpec((rank, width), lambda i, me: (0, 0)),
            ],
            out_specs=[pl.BlockSpec(shape, lambda i, me: (0, 0, 0))] * 4,
        ),
        compiler_params=pltpu.CompilerParams(vmem_limit_bytes=vmem_limit),
        cost_estimate=pl.CostEstimate(
            flops=0,
            bytes_accessed=0,
            transcendentals=0,
        ),
    )(me, inner_emb, basis)


def emb_base_body(outer_ref, moment_ref, basis_ref, base_ref, proj_ref):
    shape = base_ref.shape
    outer = outer_ref[0, :, 0].reshape(-1, shape[-1])
    moment = moment_ref[0, :, 0].reshape(-1, shape[-1])
    basis = basis_ref[...]
    proj = mul_t(outer, basis)
    proj_ref[...] = proj
    base = outer - moment_weight * moment - grad_weight * mul(proj, basis)
    base_ref[...] = base.reshape(shape)


def emb_block_body(scale, base_ref, p0, p1, p2, p3, basis_ref, block_ref, sum_ref):
    total = p0[...] + p1[...] + p2[...] + p3[...]
    sum_ref[...] = total
    pieces, half, wide = total.shape
    flat = total.reshape(pieces * half, wide)
    first, second = wide_basis(basis_ref[...])
    base = base_ref[...]
    block_ref[:, 0] = base[:, 0] + scale * mul(flat, first).reshape(pieces, half, -1)
    block_ref[:, 1] = base[:, 1] + scale * mul(flat, second).reshape(pieces, half, -1)


def emb_state_body(scale, outer_ref, moment_ref, proj_ref, back_ref, basis_ref, new_ref, moment_new_ref):
    pieces, half, wide = back_ref.shape
    basis = basis_ref[...]
    first, second = wide_basis(basis)
    flat = back_ref[...].reshape(pieces * half, wide)
    outer = outer_ref[0, :, 0]
    width = outer.shape[-1]
    own = mul(proj_ref[...], basis).reshape(pieces, 2, half, width)
    grad = jnp.concatenate(
        [
            own[:, i : i + 1] - scale * mul(flat, part).reshape(pieces, 1, half, width)
            for i, part in ((0, first), (1, second))
        ],
        axis=1,
    ).reshape(outer.shape)
    moment_new = momentum * moment_ref[0, :, 0] + grad
    moment_new_ref[0, :, 0] = moment_new
    new_ref[0, :, 0] = outer - outer_rate * (grad + momentum * moment_new)


def per_device(inner_dense, inner_emb, outer_dense, moment_dense, outer_emb, moment_emb, basis):
    groups = lax.axis_size("rep")
    tp_count = lax.axis_size("tp")
    me = lax.axis_index("rep")

    def send(x, d):
        return lax.ppermute(x, "rep", [(i, i ^ d) for i in range(groups)])

    def meet(*xs):
        return lax.optimization_barrier(xs)

    def swap(x):
        return lax.all_to_all(x, "tp", split_axis=0, concat_axis=0, tiled=True)

    rank, width = basis.shape
    dense = inner_dense[0]
    cols = dense.shape[2]
    block_rows = dense.shape[1] // groups
    flat_rows = outer_dense.shape[2]
    piece_rows = outer_emb.shape[3]
    half_rows = piece_rows // 2
    emb_rows = tp_count * piece_rows
    weight = grad_weight / groups

    def block(d):
        return lax.dynamic_slice(dense, (0, (me ^ d) * block_rows, 0), (2, block_rows, cols))

    far, inner_emb, outer_emb, outer_dense, dense = meet(
        block(3), inner_emb, outer_emb, outer_dense, dense
    )
    far = send(far, 1)

    p3, p2, p1, p0 = project(inner_emb, basis, me.reshape(1).astype(jnp.int32), groups, tp_count)
    p3, p2, p1, p0, outer_emb = meet(p3, p2, p1, p0, outer_emb)
    p3, p2, p1 = send(p3, 3), send(p2, 2), send(p1, 1)
    emb_base, outer_proj = call(
        emb_base_body,
        [shaped(tp_count, piece_rows, width), shaped(emb_rows, rank)],
        3,
        flops=24 * emb_rows * width * rank,
        size=12 * emb_rows * width,
    )(outer_emb, moment_emb, basis)
    own, near, second = block(0), block(1), block(2)
    far, emb_base, near = meet(far, emb_base, near)
    emb_base = swap(emb_base)
    across = send(second + far, 2)
    near = send(near, 1)
    dense_outer = outer_dense[:, 0]
    dense_moment = moment_dense[:, 0]
    dense_base = (1.0 - grad_weight) * dense_outer - moment_weight * dense_moment
    dense_base = jnp.stack([dense_base[:, :, j * cols : (j + 1) * cols] for j in range(tp_count)])

    emb_block, proj_sum = call(
        functools.partial(emb_block_body, weight),
        [shaped(tp_count, 2, half_rows, width), shaped(tp_count, half_rows, 2 * rank)],
        6,
        flops=24 * emb_rows * width * rank,
        size=8 * emb_rows * width,
    )(emb_base.reshape(tp_count, 2, half_rows, width), p0, p1, p2, p3, basis)
    emb_block, proj_sum, dense_base = meet(emb_block, proj_sum, dense_base)
    dense_base = swap(dense_base)
    across, near, emb_block = meet(across, near, emb_block)
    dense_sum = own + near + across
    emb_block = emb_block.reshape(emb_rows, width)
    dense_block = (
        dense_base.transpose(1, 0, 2, 3).reshape(2, block_rows, cols) + weight * dense_sum
    )

    def gather(x):
        second = send(x, 2)
        first = send(x, 1)
        return x, first, second, send(second, 1)

    emb_second, emb_first = send(emb_block, 2), send(emb_block, 1)
    dense_second, dense_first = send(dense_block, 2), send(dense_block, 1)
    emb_fwd, dense_fwd = emb_second, dense_second
    emb_far = send(emb_fwd, 1)
    dense_far = send(dense_fwd, 1)
    emb_all = (emb_block, emb_first, emb_second, emb_far)
    dense_all = (dense_block, dense_first, dense_second, dense_far)
    embed_train = jnp.zeros((groups * emb_rows, width), f32)
    for d, value in enumerate(emb_all):
        embed_train = lax.dynamic_update_slice(embed_train, value, ((me ^ d) * emb_rows, 0))
    dense_train = jnp.zeros(dense.shape, f32)
    for d, value in enumerate(dense_all):
        dense_train = lax.dynamic_update_slice(dense_train, value, (0, (me ^ d) * block_rows, 0))

    dense_back = swap(dense_sum.reshape(2, tp_count, flat_rows, cols).transpose(1, 0, 2, 3))
    dense_back = jnp.concatenate([dense_back[j] for j in range(tp_count)], axis=-1)
    grad_dense = dense_outer - dense_back / groups
    moment_new = momentum * dense_moment + grad_dense
    dense_new = dense_outer - outer_rate * (grad_dense + momentum * moment_new)
    emb_new, emb_moment_new = call(
        functools.partial(emb_state_body, 1.0 / groups),
        [shaped(*outer_emb.shape)] * 2,
        5,
        flops=36 * emb_rows * width * rank,
        size=16 * emb_rows * width,
    )(outer_emb, moment_emb, outer_proj, swap(proj_sum), basis)
    return (
        dense_new[:, None],
        moment_new[:, None],
        emb_new,
        emb_moment_new,
        dense_train,
        embed_train,
    )


def solution(mesh):
    in_specs = (
        P("rep", None, "shard", "tp"),
        P("rep", ("shard", "tp"), None),
        P(None, "shard", ("rep", "tp"), None),
        P(None, "shard", ("rep", "tp"), None),
        P("shard", None, ("rep", "tp"), None, None),
        P("shard", None, ("rep", "tp"), None, None),
        P(),
    )
    out_specs = (
        P(None, "shard", ("rep", "tp"), None),
        P(None, "shard", ("rep", "tp"), None),
        P("shard", None, ("rep", "tp"), None, None),
        P("shard", None, ("rep", "tp"), None, None),
        P(None, "shard", "tp"),
        P(("shard", "tp"), None),
    )
    return jax.shard_map(
        per_device, mesh=mesh, in_specs=in_specs, out_specs=out_specs, check_vma=False
    )
```

```python
import functools

import jax
import jax.numpy as jnp
from jax import lax
from jax.experimental import pallas as pl
from jax.experimental.pallas import tpu as pltpu
from jax.sharding import PartitionSpec as P

momentum = 0.9
outer_rate = 0.7
grad_weight = outer_rate * (1.0 + momentum)
moment_weight = outer_rate * momentum * momentum
vmem_limit = 48 * 1024 * 1024
f32 = jnp.float32
any_spec = pl.BlockSpec(memory_space=pl.ANY)
vmem_spec = pl.BlockSpec(memory_space=pltpu.VMEM)


def mul_t(a, b):
    return lax.dot_general(
        a, b, (((1,), (1,)), ((), ())), precision=lax.Precision.HIGHEST, preferred_element_type=f32
    )


def mul(a, b):
    return jnp.dot(a, b, precision=lax.Precision.HIGHEST, preferred_element_type=f32)


def shaped(*shape):
    return jax.ShapeDtypeStruct(shape, f32)


def call(body, outs, n_in, scratch=(), flops=0, size=0):
    return pl.pallas_call(
        body,
        out_shape=outs,
        in_specs=[vmem_spec] * n_in,
        out_specs=jax.tree.map(lambda _: vmem_spec, outs),
        scratch_shapes=scratch,
        compiler_params=pltpu.CompilerParams(vmem_limit_bytes=vmem_limit),
        cost_estimate=pl.CostEstimate(flops=0, bytes_accessed=0, transcendentals=0),
    )


def wide_basis(basis):
    zero = jnp.zeros_like(basis)
    return jnp.concatenate([basis, zero]), jnp.concatenate([zero, basis])


def project_body(count, groups, pieces, me_ref, x_ref, basis_ref, *out_refs):
    step = pl.program_id(0)
    first, second = wide_basis(basis_ref[...])
    rows, width = x_ref.shape[1:]
    x = x_ref[0].reshape(pieces, 2, rows // pieces // 2, width)
    y = mul_t(x[:, 0].reshape(-1, width), first) + mul_t(x[:, 1].reshape(-1, width), second)
    y = y.reshape(pieces, rows // pieces // 2, -1)
    for i in range(count):

        @pl.when(step == i)
        def _(i=i):
            out_refs[i][...] = y


def project(inner_emb, basis, me, groups, pieces):
    rows, width = inner_emb.shape[1] // groups, inner_emb.shape[2]
    rank = basis.shape[0]
    shape = (pieces, rows // pieces // 2, 2 * rank)

    def source(i, me):
        return 0, me[0] ^ (groups - 1 - i), 0

    return pl.pallas_call(
        functools.partial(project_body, 4, groups, pieces),
        out_shape=[shaped(*shape)] * 4,
        grid_spec=pltpu.PrefetchScalarGridSpec(
            num_scalar_prefetch=1,
            grid=(4,),
            in_specs=[
                pl.BlockSpec((1, rows, width), source),
                pl.BlockSpec((rank, width), lambda i, me: (0, 0)),
            ],
            out_specs=[pl.BlockSpec(shape, lambda i, me: (0, 0, 0))] * 4,
        ),
        compiler_params=pltpu.CompilerParams(vmem_limit_bytes=vmem_limit),
        cost_estimate=pl.CostEstimate(
            flops=0,
            bytes_accessed=0,
            transcendentals=0,
        ),
    )(me, inner_emb, basis)


def emb_base_body(outer_ref, moment_ref, basis_ref, base_ref, proj_ref):
    shape = base_ref.shape
    outer = outer_ref[0, :, 0].reshape(-1, shape[-1])
    moment = moment_ref[0, :, 0].reshape(-1, shape[-1])
    basis = basis_ref[...]
    proj = mul_t(outer, basis)
    proj_ref[...] = proj
    base = outer - moment_weight * moment - grad_weight * mul(proj, basis)
    base_ref[...] = base.reshape(shape)


def emb_block_body(scale, base_ref, p0, p1, p2, p3, basis_ref, block_ref, sum_ref):
    total = p0[...] + p1[...] + p2[...] + p3[...]
    sum_ref[...] = total
    pieces, half, wide = total.shape
    flat = total.reshape(pieces * half, wide)
    first, second = wide_basis(basis_ref[...])
    base = base_ref[...]
    block_ref[:, 0] = base[:, 0] + scale * mul(flat, first).reshape(pieces, half, -1)
    block_ref[:, 1] = base[:, 1] + scale * mul(flat, second).reshape(pieces, half, -1)


def emb_state_body(scale, outer_ref, moment_ref, proj_ref, back_ref, basis_ref, new_ref, moment_new_ref):
    pieces, half, wide = back_ref.shape
    basis = basis_ref[...]
    first, second = wide_basis(basis)
    flat = back_ref[...].reshape(pieces * half, wide)
    outer = outer_ref[0, :, 0]
    width = outer.shape[-1]
    own = mul(proj_ref[...], basis).reshape(pieces, 2, half, width)
    grad = jnp.concatenate(
        [
            own[:, i : i + 1] - scale * mul(flat, part).reshape(pieces, 1, half, width)
            for i, part in ((0, first), (1, second))
        ],
        axis=1,
    ).reshape(outer.shape)
    moment_new = momentum * moment_ref[0, :, 0] + grad
    moment_new_ref[0, :, 0] = moment_new
    new_ref[0, :, 0] = outer - outer_rate * (grad + momentum * moment_new)


def per_device(inner_dense, inner_emb, outer_dense, moment_dense, outer_emb, moment_emb, basis):
    groups = lax.axis_size("rep")
    tp_count = lax.axis_size("tp")
    me = lax.axis_index("rep")

    def send(x, d):
        return lax.ppermute(x, "rep", [(i, i ^ d) for i in range(groups)])

    def meet(*xs):
        return lax.optimization_barrier(xs)

    def swap(x):
        return lax.all_to_all(x, "tp", split_axis=0, concat_axis=0, tiled=True)

    rank, width = basis.shape
    dense = inner_dense[0]
    cols = dense.shape[2]
    block_rows = dense.shape[1] // groups
    flat_rows = outer_dense.shape[2]
    piece_rows = outer_emb.shape[3]
    half_rows = piece_rows // 2
    emb_rows = tp_count * piece_rows
    weight = grad_weight / groups

    def block(d):
        return lax.dynamic_slice(dense, (0, (me ^ d) * block_rows, 0), (2, block_rows, cols))

    def half(d, h):
        return lax.dynamic_slice(dense, (h, (me ^ d) * block_rows, 0), (1, block_rows, cols))

    low, high, inner_emb, outer_emb, outer_dense, dense = meet(
        jnp.concatenate([half(3, 0), half(1, 0)]),
        jnp.concatenate([half(2, 1), half(3, 1)]),
        inner_emb,
        outer_emb,
        outer_dense,
        dense,
    )
    low, high = send(low, 1), send(high, 2)

    p3, p2, p1, p0 = project(inner_emb, basis, me.reshape(1).astype(jnp.int32), groups, tp_count)
    p3, p2, p1, p0, outer_emb = meet(p3, p2, p1, p0, outer_emb)
    p3, p2, p1 = send(p3, 3), send(p2, 2), send(p1, 1)
    emb_base, outer_proj = call(
        emb_base_body,
        [shaped(tp_count, piece_rows, width), shaped(emb_rows, rank)],
        3,
        flops=24 * emb_rows * width * rank,
        size=12 * emb_rows * width,
    )(outer_emb, moment_emb, basis)
    own = block(0)
    low, emb_base = meet(low, emb_base)
    emb_base = swap(emb_base)
    across = send(half(2, 0) + low[:1], 2)
    near = send(half(1, 1) + high[1:], 1)
    dense_outer = outer_dense[:, 0]
    dense_moment = moment_dense[:, 0]
    dense_base = (1.0 - grad_weight) * dense_outer - moment_weight * dense_moment
    dense_base = jnp.stack([dense_base[:, :, j * cols : (j + 1) * cols] for j in range(tp_count)])

    emb_block, proj_sum = call(
        functools.partial(emb_block_body, weight),
        [shaped(tp_count, 2, half_rows, width), shaped(tp_count, half_rows, 2 * rank)],
        6,
        flops=24 * emb_rows * width * rank,
        size=8 * emb_rows * width,
    )(emb_base.reshape(tp_count, 2, half_rows, width), p0, p1, p2, p3, basis)
    emb_block, proj_sum, dense_base = meet(emb_block, proj_sum, dense_base)
    dense_base = swap(dense_base)
    across, near, emb_block = meet(across, near, emb_block)
    dense_sum = own + jnp.concatenate([low[1:] + across, high[:1] + near])
    emb_block = emb_block.reshape(emb_rows, width)
    dense_block = (
        dense_base.transpose(1, 0, 2, 3).reshape(2, block_rows, cols) + weight * dense_sum
    )

    def gather(x):
        second = send(x, 2)
        first = send(x, 1)
        return x, first, second, send(second, 1)

    emb_second, emb_first = send(emb_block, 2), send(emb_block, 1)
    dense_second, dense_first = send(dense_block, 2), send(dense_block, 1)
    emb_fwd, dense_fwd = emb_second, dense_second
    emb_far = send(emb_fwd, 1)
    dense_far = send(dense_fwd, 1)
    emb_all = (emb_block, emb_first, emb_second, emb_far)
    dense_all = (dense_block, dense_first, dense_second, dense_far)
    embed_train = jnp.zeros((groups * emb_rows, width), f32)
    for d, value in enumerate(emb_all):
        embed_train = lax.dynamic_update_slice(embed_train, value, ((me ^ d) * emb_rows, 0))
    dense_train = jnp.zeros(dense.shape, f32)
    for d, value in enumerate(dense_all):
        dense_train = lax.dynamic_update_slice(dense_train, value, (0, (me ^ d) * block_rows, 0))

    dense_back = swap(dense_sum.reshape(2, tp_count, flat_rows, cols).transpose(1, 0, 2, 3))
    dense_back = jnp.concatenate([dense_back[j] for j in range(tp_count)], axis=-1)
    grad_dense = dense_outer - dense_back / groups
    moment_new = momentum * dense_moment + grad_dense
    dense_new = dense_outer - outer_rate * (grad_dense + momentum * moment_new)
    emb_new, emb_moment_new = call(
        functools.partial(emb_state_body, 1.0 / groups),
        [shaped(*outer_emb.shape)] * 2,
        5,
        flops=36 * emb_rows * width * rank,
        size=16 * emb_rows * width,
    )(outer_emb, moment_emb, outer_proj, swap(proj_sum), basis)
    return (
        dense_new[:, None],
        moment_new[:, None],
        emb_new,
        emb_moment_new,
        dense_train,
        embed_train,
    )


def solution(mesh):
    in_specs = (
        P("rep", None, "shard", "tp"),
        P("rep", ("shard", "tp"), None),
        P(None, "shard", ("rep", "tp"), None),
        P(None, "shard", ("rep", "tp"), None),
        P("shard", None, ("rep", "tp"), None, None),
        P("shard", None, ("rep", "tp"), None, None),
        P(),
    )
    out_specs = (
        P(None, "shard", ("rep", "tp"), None),
        P(None, "shard", ("rep", "tp"), None),
        P("shard", None, ("rep", "tp"), None, None),
        P("shard", None, ("rep", "tp"), None, None),
        P(None, "shard", "tp"),
        P(("shard", "tp"), None),
    )
    return jax.shard_map(
        per_device, mesh=mesh, in_specs=in_specs, out_specs=out_specs, check_vma=False
    )
```

```python
import functools

import jax
import jax.numpy as jnp
from jax import lax
from jax.experimental import pallas as pl
from jax.experimental.pallas import tpu as pltpu
from jax.sharding import PartitionSpec as P

momentum = 0.9
outer_rate = 0.7
grad_weight = outer_rate * (1.0 + momentum)
moment_weight = outer_rate * momentum * momentum
vmem_limit = 48 * 1024 * 1024
f32 = jnp.float32
any_spec = pl.BlockSpec(memory_space=pl.ANY)
vmem_spec = pl.BlockSpec(memory_space=pltpu.VMEM)


def mul_t(a, b):
    return lax.dot_general(
        a, b, (((1,), (1,)), ((), ())), precision=lax.Precision.HIGHEST, preferred_element_type=f32
    )


def mul(a, b):
    return jnp.dot(a, b, precision=lax.Precision.HIGHEST, preferred_element_type=f32)


def shaped(*shape):
    return jax.ShapeDtypeStruct(shape, f32)


def call(body, outs, n_in, scratch=(), flops=0, size=0):
    return pl.pallas_call(
        body,
        out_shape=outs,
        in_specs=[vmem_spec] * n_in,
        out_specs=jax.tree.map(lambda _: vmem_spec, outs),
        scratch_shapes=scratch,
        compiler_params=pltpu.CompilerParams(vmem_limit_bytes=vmem_limit),
        cost_estimate=pl.CostEstimate(flops=0, bytes_accessed=0, transcendentals=0),
    )


def wide_basis(basis):
    zero = jnp.zeros_like(basis)
    return jnp.concatenate([basis, zero]), jnp.concatenate([zero, basis])


def project_body(count, groups, pieces, me_ref, x_ref, basis_ref, *out_refs):
    step = pl.program_id(0)
    first, second = wide_basis(basis_ref[...])
    rows, width = x_ref.shape[1:]
    x = x_ref[0].reshape(pieces, 2, rows // pieces // 2, width)
    y = mul_t(x[:, 0].reshape(-1, width), first) + mul_t(x[:, 1].reshape(-1, width), second)
    y = y.reshape(pieces, rows // pieces // 2, -1)
    for i in range(count):

        @pl.when(step == i)
        def _(i=i):
            out_refs[i][...] = y


def project(inner_emb, basis, me, groups, pieces):
    rows, width = inner_emb.shape[1] // groups, inner_emb.shape[2]
    rank = basis.shape[0]
    shape = (pieces, rows // pieces // 2, 2 * rank)

    def source(i, me):
        return 0, me[0] ^ (groups - 1 - i), 0

    return pl.pallas_call(
        functools.partial(project_body, 4, groups, pieces),
        out_shape=[shaped(*shape)] * 4,
        grid_spec=pltpu.PrefetchScalarGridSpec(
            num_scalar_prefetch=1,
            grid=(4,),
            in_specs=[
                pl.BlockSpec((1, rows, width), source),
                pl.BlockSpec((rank, width), lambda i, me: (0, 0)),
            ],
            out_specs=[pl.BlockSpec(shape, lambda i, me: (0, 0, 0))] * 4,
        ),
        compiler_params=pltpu.CompilerParams(vmem_limit_bytes=vmem_limit),
        cost_estimate=pl.CostEstimate(
            flops=0,
            bytes_accessed=0,
            transcendentals=0,
        ),
    )(me, inner_emb, basis)


def emb_base_body(outer_ref, moment_ref, basis_ref, base_ref, proj_ref):
    shape = base_ref.shape
    outer = outer_ref[0, :, 0].reshape(-1, shape[-1])
    moment = moment_ref[0, :, 0].reshape(-1, shape[-1])
    basis = basis_ref[...]
    proj = mul_t(outer, basis)
    proj_ref[...] = proj
    base = outer - moment_weight * moment - grad_weight * mul(proj, basis)
    base_ref[...] = base.reshape(shape)


def emb_block_body(scale, base_ref, p0, p1, p2, p3, basis_ref, block_ref, sum_ref):
    total = p0[...] + p1[...] + p2[...] + p3[...]
    sum_ref[...] = total
    pieces, half, wide = total.shape
    flat = total.reshape(pieces * half, wide)
    first, second = wide_basis(basis_ref[...])
    base = base_ref[...]
    block_ref[:, 0] = base[:, 0] + scale * mul(flat, first).reshape(pieces, half, -1)
    block_ref[:, 1] = base[:, 1] + scale * mul(flat, second).reshape(pieces, half, -1)


def emb_state_body(scale, outer_ref, moment_ref, proj_ref, back_ref, basis_ref, new_ref, moment_new_ref):
    pieces, half, wide = back_ref.shape
    basis = basis_ref[...]
    first, second = wide_basis(basis)
    flat = back_ref[...].reshape(pieces * half, wide)
    outer = outer_ref[0, :, 0]
    width = outer.shape[-1]
    own = mul(proj_ref[...], basis).reshape(pieces, 2, half, width)
    grad = jnp.concatenate(
        [
            own[:, i : i + 1] - scale * mul(flat, part).reshape(pieces, 1, half, width)
            for i, part in ((0, first), (1, second))
        ],
        axis=1,
    ).reshape(outer.shape)
    moment_new = momentum * moment_ref[0, :, 0] + grad
    moment_new_ref[0, :, 0] = moment_new
    new_ref[0, :, 0] = outer - outer_rate * (grad + momentum * moment_new)


def per_device(inner_dense, inner_emb, outer_dense, moment_dense, outer_emb, moment_emb, basis):
    groups = lax.axis_size("rep")
    tp_count = lax.axis_size("tp")
    me = lax.axis_index("rep")

    def send(x, d):
        return lax.ppermute(x, "rep", [(i, i ^ d) for i in range(groups)])

    def meet(*xs):
        return lax.optimization_barrier(xs)

    def swap(x):
        return lax.all_to_all(x, "tp", split_axis=0, concat_axis=0, tiled=True)

    rank, width = basis.shape
    dense = inner_dense[0]
    cols = dense.shape[2]
    block_rows = dense.shape[1] // groups
    flat_rows = outer_dense.shape[2]
    piece_rows = outer_emb.shape[3]
    half_rows = piece_rows // 2
    emb_rows = tp_count * piece_rows
    weight = grad_weight / groups

    def block(d):
        return lax.dynamic_slice(dense, (0, (me ^ d) * block_rows, 0), (2, block_rows, cols))

    def half(d, h):
        return lax.dynamic_slice(dense, (h, (me ^ d) * block_rows, 0), (1, block_rows, cols))

    low, high, inner_emb, outer_emb, outer_dense, dense = meet(
        jnp.concatenate([half(3, 0), half(1, 0)]),
        jnp.concatenate([half(2, 1), half(3, 1)]),
        inner_emb,
        outer_emb,
        outer_dense,
        dense,
    )
    low, high = send(low, 1), send(high, 2)

    p3, p2, p1, p0 = project(inner_emb, basis, me.reshape(1).astype(jnp.int32), groups, tp_count)
    p3, p2, p1, p0, outer_emb = meet(p3, p2, p1, p0, outer_emb)
    p3, p2, p1 = send(p3, 3), send(p2, 2), send(p1, 1)
    emb_base, outer_proj = call(
        emb_base_body,
        [shaped(tp_count, piece_rows, width), shaped(emb_rows, rank)],
        3,
        flops=24 * emb_rows * width * rank,
        size=12 * emb_rows * width,
    )(outer_emb, moment_emb, basis)
    own = block(0)
    low, emb_base = meet(low, emb_base)
    emb_base = swap(emb_base)
    across = send(half(2, 0) + low[:1], 2)
    near = send(half(1, 1) + high[1:], 1)
    dense_outer = outer_dense[:, 0]
    dense_moment = moment_dense[:, 0]
    dense_base = (1.0 - grad_weight) * dense_outer - moment_weight * dense_moment
    dense_base = jnp.stack([dense_base[:, :, j * cols : (j + 1) * cols] for j in range(tp_count)])

    emb_block, proj_sum = call(
        functools.partial(emb_block_body, weight),
        [shaped(tp_count, 2, half_rows, width), shaped(tp_count, half_rows, 2 * rank)],
        6,
        flops=24 * emb_rows * width * rank,
        size=8 * emb_rows * width,
    )(emb_base.reshape(tp_count, 2, half_rows, width), p0, p1, p2, p3, basis)
    emb_block, proj_sum, dense_base = meet(emb_block, proj_sum, dense_base)
    dense_base = swap(dense_base)
    near, emb_block = meet(near, emb_block)
    dense_sum = own + jnp.concatenate([low[1:] + across, high[:1] + near])
    emb_block = emb_block.reshape(emb_rows, width)
    dense_block = (
        dense_base.transpose(1, 0, 2, 3).reshape(2, block_rows, cols) + weight * dense_sum
    )

    def gather(x):
        second = send(x, 2)
        first = send(x, 1)
        return x, first, second, send(second, 1)

    emb_second, emb_first = send(emb_block, 2), send(emb_block, 1)
    dense_second, dense_first = send(dense_block, 2), send(dense_block, 1)
    emb_fwd, dense_fwd = emb_second, dense_second
    emb_far = send(emb_fwd, 1)
    dense_far = send(dense_fwd, 1)
    emb_all = (emb_block, emb_first, emb_second, emb_far)
    dense_all = (dense_block, dense_first, dense_second, dense_far)
    embed_train = jnp.zeros((groups * emb_rows, width), f32)
    for d, value in enumerate(emb_all):
        embed_train = lax.dynamic_update_slice(embed_train, value, ((me ^ d) * emb_rows, 0))
    dense_train = jnp.zeros(dense.shape, f32)
    for d, value in enumerate(dense_all):
        dense_train = lax.dynamic_update_slice(dense_train, value, (0, (me ^ d) * block_rows, 0))

    dense_back = swap(dense_sum.reshape(2, tp_count, flat_rows, cols).transpose(1, 0, 2, 3))
    dense_back = jnp.concatenate([dense_back[j] for j in range(tp_count)], axis=-1)
    grad_dense = dense_outer - dense_back / groups
    moment_new = momentum * dense_moment + grad_dense
    dense_new = dense_outer - outer_rate * (grad_dense + momentum * moment_new)
    emb_new, emb_moment_new = call(
        functools.partial(emb_state_body, 1.0 / groups),
        [shaped(*outer_emb.shape)] * 2,
        5,
        flops=36 * emb_rows * width * rank,
        size=16 * emb_rows * width,
    )(outer_emb, moment_emb, outer_proj, swap(proj_sum), basis)
    return (
        dense_new[:, None],
        moment_new[:, None],
        emb_new,
        emb_moment_new,
        dense_train,
        embed_train,
    )


def solution(mesh):
    in_specs = (
        P("rep", None, "shard", "tp"),
        P("rep", ("shard", "tp"), None),
        P(None, "shard", ("rep", "tp"), None),
        P(None, "shard", ("rep", "tp"), None),
        P("shard", None, ("rep", "tp"), None, None),
        P("shard", None, ("rep", "tp"), None, None),
        P(),
    )
    out_specs = (
        P(None, "shard", ("rep", "tp"), None),
        P(None, "shard", ("rep", "tp"), None),
        P("shard", None, ("rep", "tp"), None, None),
        P("shard", None, ("rep", "tp"), None, None),
        P(None, "shard", "tp"),
        P(("shard", "tp"), None),
    )
    return jax.shard_map(
        per_device, mesh=mesh, in_specs=in_specs, out_specs=out_specs, check_vma=False
    )
```
